32 devices in a mesh: seq: 8 (over z, y), dp: 4 (over x, core).
Axes of the slice: x: 2, y: 2, z: 4, core: 2. Of those that a mesh axis runs over, the one named last changes fastest.
Arguments:
- queries: bfloat16 [4, 4096, 1024], P('dp', 'seq'), may hold values from -8 to 8
- memory_keys: bfloat16 [4, 4096, 1024], P('dp', 'seq'), may hold values from -8 to 8
- memory_values: bfloat16 [4, 4096, 1024], P('dp', 'seq'), may hold values from -6 to 6
- out_weight: bfloat16 [1024, 2048], P('seq'), may hold values from -0.1875 to 0.1875
- grad_out: bfloat16 [4, 4096, 2048], P('dp', 'seq'), may hold values from -6 to 6
- key_first: int32 [4, 32], P('dp', 'seq'), may hold values from 0 to 30, as said below
- key_last: int32 [4, 32], P('dp', 'seq'), may hold values from 2 to 32
Outputs:
- layer_out: bfloat16 [4, 4096, 2048], P('dp', 'seq')
- grad_query: bfloat16 [4, 4096, 1024], P('dp', 'seq')
- grad_keys: bfloat16 [4, 4096, 1024], P('dp', 'seq')
- grad_values: bfloat16 [4, 4096, 1024], P('dp', 'seq')
- weight_grad: float32 [1024, 2048], P('seq')
The draws below stay inside these ranges and needn't reach their ends.
Inputs may be any that keep to these rules, and one draw needn't show every extreme that they name: With key_last: query block b of pack p attends to key blocks key_first[p, b] to key_last[p, b] - 1, blocks of 128 tokens. Sentence pairs tile aligned groups of 4 blocks that begin at block 2, the first and last groups holding 4 // 2 blocks; a query block's key blocks lie in its own group and number 1 to 3, 3 in some group of every pack.
All inputs are finite; a program needn't handle non-finite values.
Results may differ from the reference program's by a relative error of at most 0.0095.
Values may be sent and summed in bfloat16 or wider, within the bound.
No kernel may reach another device: no remote copies, remote signals or barrier semaphores. Data moves between devices by JAX's collectives and lax.ppermute only.
A program may use at most 192 MiB of HBM per device.

```python
import math
import jax
import jax.numpy as jnp
from jax import lax

D = 2048
HDIM = 128
HEADS = 8
BLOCK = 128
GROUP = 4
HD = 1024
SPAN = 3
TOKENS = 4096
QBLOCKS = 32
PACKS = 4


def pair_layout(key):
    inner_groups = QBLOCKS // GROUP - 1
    half_group = GROUP // 2
    split_query = jax.random.randint(jax.random.fold_in(key, 3), (PACKS, inner_groups), 1, GROUP)
    split_key = jax.random.randint(jax.random.fold_in(key, 4), (PACKS, inner_groups), 1, GROUP)
    split_key = split_key.at[:, 0].set(GROUP - 1)
    blocks = jnp.arange(QBLOCKS, dtype=jnp.int32)
    group_index = jnp.clip((blocks - half_group) // GROUP, 0, inner_groups - 1)
    within = blocks - half_group - group_index * GROUP
    group_start = half_group + group_index * GROUP
    query_split = split_query[:, group_index]
    key_split = split_key[:, group_index]
    early = within[None, :] < query_split
    first_block = jnp.where(early, group_start[None, :], group_start[None, :] + key_split)
    last_block = jnp.where(early, group_start[None, :] + key_split, group_start[None, :] + GROUP)
    leading = (blocks < half_group)[None, :]
    trailing = (blocks >= QBLOCKS - half_group)[None, :]
    first_block = jnp.where(leading, 0, jnp.where(trailing, QBLOCKS - half_group, first_block))
    last_block = jnp.where(leading, half_group, jnp.where(trailing, QBLOCKS, last_block))
    return (first_block.astype(jnp.int32), last_block.astype(jnp.int32))


def draw_key_first(key, part):
    return pair_layout(jax.random.fold_in(key, 1))[0]


def draw_key_last(key, part):
    return pair_layout(jax.random.fold_in(key, 1))[1]


def draw_queries(key, part):
    sample = jax.random.truncated_normal(jax.random.fold_in(key, 21), -4.0, 4.0, (PACKS, TOKENS, HD), jnp.float32)
    return sample.astype(jnp.bfloat16)


def draw_memory_keys(key, part):
    sample = jax.random.truncated_normal(jax.random.fold_in(key, 22), -4.0, 4.0, (PACKS, TOKENS, HD), jnp.float32)
    return sample.astype(jnp.bfloat16)


def level_of(rng, shape, pieces, low, top_value):
    gain, own = 1.0, jax.random.fold_in(rng, 6)
    for dim, parts in pieces:
        heights = jnp.exp(jax.random.uniform(jax.random.fold_in(own, dim), (parts,), jnp.float32, low / len(pieces), top_value / len(pieces)))
        gain = gain * jnp.repeat(heights, shape[dim] // parts).reshape([-1 if axis == dim else 1 for axis in range(len(shape))])
    return gain


def noise(key, extent, deviation, bound, split=(), kind=jnp.bfloat16):
    values = deviation * jax.random.normal(key, extent, jnp.float32)
    if split:
        values = values * level_of(key, extent, split, -0.22, 0.18)
    return jnp.clip(values, -bound, bound).astype(kind)


def setup_inputs(seed: int = 0) -> dict:
    streams_of = jax.random.split(jax.random.key(seed), 8)
    return {
        "queries": draw_queries(jax.random.fold_in(streams_of[7], 71), 0),
        "memory_keys": draw_memory_keys(jax.random.fold_in(streams_of[7], 71), 0),
        "memory_values": noise(streams_of[2], (PACKS, TOKENS, HD), 1.0, 6.0, ((0, 4), (1, 8))),
        "out_weight": noise(streams_of[3], (HD, D), HD ** -0.5, 0.1875, ((0, 8),)),
        "grad_out": noise(streams_of[4], (PACKS, TOKENS, D), 1.0, 6.0, ((0, 4), (1, 8))),
        "key_first": draw_key_first(jax.random.fold_in(streams_of[7], 71), 0),
        "key_last": draw_key_last(jax.random.fold_in(streams_of[7], 71), 0),
    }


def attend_block(query_rows, key_rows, value_rows, grad_rows, allowed):
    score_scale = 1.0 / math.sqrt(HDIM)
    query_heads = query_rows.reshape(BLOCK, HEADS, HDIM).astype(jnp.float32)
    key_heads = key_rows.reshape(-1, HEADS, HDIM).astype(jnp.float32)
    value_heads = value_rows.reshape(-1, HEADS, HDIM).astype(jnp.float32)
    grad_heads = grad_rows.reshape(BLOCK, HEADS, HDIM).astype(jnp.float32)
    scores = jnp.einsum('qhd,khd->hqk', query_heads, key_heads) * score_scale
    inside = allowed[None, None, :]
    highest = lax.optimization_barrier(jnp.max(jnp.where(inside, scores, -jnp.inf), axis=-1, keepdims=True))
    raised = jnp.where(inside, jnp.exp(scores - highest), 0.0)
    softmax_probs = raised / lax.optimization_barrier(jnp.sum(raised, axis=-1, keepdims=True))
    weights = lax.optimization_barrier(softmax_probs.astype(jnp.bfloat16)).astype(jnp.float32)
    attended = jnp.einsum('hqk,khd->qhd', weights, value_heads).astype(jnp.bfloat16)
    grad_probs = jnp.einsum('qhd,khd->hqk', grad_heads, value_heads)
    row_term = lax.optimization_barrier(jnp.sum(softmax_probs * grad_probs, axis=-1, keepdims=True))
    grad_scores = (softmax_probs * (grad_probs - row_term) * score_scale).astype(jnp.bfloat16)
    grad_scores = lax.optimization_barrier(grad_scores).astype(jnp.float32)
    grad_query = jnp.einsum('hqk,khd->qhd', grad_scores, key_heads).astype(jnp.bfloat16)
    key_part = jnp.einsum('hqk,qhd->khd', grad_scores, query_heads)
    value_part = jnp.einsum('hqk,qhd->khd', weights, grad_heads)
    return (attended.reshape(BLOCK, HD), grad_query.reshape(BLOCK, HD), key_part.reshape(-1, HD), value_part.reshape(-1, HD))

def one_pack(packed):
    pack_queries, pack_keys, pack_values, pack_grads, pack_first, pack_last = packed
    window_rows = SPAN * BLOCK

    def advance(running, block_index):
        key_acc, value_acc = running
        first_block = pack_first[block_index]
        last_block = pack_last[block_index]
        anchor = jnp.minimum(first_block * BLOCK, TOKENS - window_rows).astype(jnp.int32)
        row_start = (block_index * BLOCK).astype(jnp.int32)
        query_rows = lax.dynamic_slice_in_dim(pack_queries, row_start, BLOCK, 0)
        grad_rows = lax.dynamic_slice_in_dim(pack_grads, row_start, BLOCK, 0)
        key_rows = lax.dynamic_slice_in_dim(pack_keys, anchor, window_rows, 0)
        value_rows = lax.dynamic_slice_in_dim(pack_values, anchor, window_rows, 0)
        block_ids = (anchor + jnp.arange(window_rows, dtype=jnp.int32)) // BLOCK
        allowed = (block_ids >= first_block) & (block_ids < last_block)
        attended, grad_query, key_part, value_part = attend_block(query_rows, key_rows, value_rows, grad_rows, allowed)
        key_acc = lax.dynamic_update_slice_in_dim(key_acc, lax.dynamic_slice_in_dim(key_acc, anchor, window_rows, 0) + key_part, anchor, 0)
        value_acc = lax.dynamic_update_slice_in_dim(value_acc, lax.dynamic_slice_in_dim(value_acc, anchor, window_rows, 0) + value_part, anchor, 0)
        return ((key_acc, value_acc), (attended, grad_query))
    empty_sum = jnp.zeros((TOKENS, HD), jnp.float32)
    sums, outputs = lax.scan(advance, (empty_sum, empty_sum), jnp.arange(QBLOCKS, dtype=jnp.int32))
    attended = outputs[0].reshape(TOKENS, HD)
    grad_query = outputs[1].reshape(TOKENS, HD)
    return (attended, grad_query, sums[0].astype(jnp.bfloat16), sums[1].astype(jnp.bfloat16))

def reference(queries, memory_keys, memory_values, out_weight, grad_out, key_first, key_last):
    flat_grad = grad_out.reshape(PACKS * TOKENS, D)
    grad_attn = lax.dot_general(flat_grad, out_weight, (((1,), (1,)), ((), ())), preferred_element_type=jnp.float32).astype(jnp.bfloat16)
    grad_attn = grad_attn.reshape(PACKS, TOKENS, HD)
    attended, grad_query, grad_keys, grad_values = lax.map(one_pack, (queries, memory_keys, memory_values, grad_attn, key_first, key_last))
    flat_attn = attended.reshape(PACKS * TOKENS, HD)
    layer_out = jnp.dot(flat_attn, out_weight, preferred_element_type=jnp.float32).astype(jnp.bfloat16)
    layer_out = layer_out.reshape(PACKS, TOKENS, D)
    weight_grad = lax.dot_general(flat_attn, flat_grad, (((0,), (0,)), ((), ())), preferred_element_type=jnp.float32) / math.sqrt(TOKENS)
    return (layer_out, grad_query, grad_keys, grad_values, weight_grad)
```

```python
import functools
import math

import jax
import jax.numpy as jnp
from jax import lax
from jax.experimental import pallas as pl
from jax.experimental.pallas import tpu as pltpu
from jax.sharding import PartitionSpec as P

HDIM = 128
BLOCK = 128
BF16 = jnp.bfloat16
F32 = jnp.float32
EXCLUDED = -1e30


def dot(a, b, contract):
    return lax.dot_general(a, b, ((contract[0], contract[1]), ((), ())), preferred_element_type=F32)


def swap(block, axis, mask):
    pairs = [(i, i ^ mask) for i in range(lax.axis_size(axis))]
    return lax.ppermute(block, axis, pairs)


def shift(block, axis, distance):
    devices = range(lax.axis_size(axis))
    return lax.ppermute(block, axis, [(i, i + distance) for i in devices if i + distance in devices])


def whole(shape):
    return pl.BlockSpec(shape, lambda *_: (0,) * len(shape))


def forward_kernel(meta, q_ref, k_ref, v_ref, low_ref, high_ref, attn_ref, prob_ref):
    rows = q_ref.shape[0]
    half = rows // 2
    blocks = rows // BLOCK
    scale = math.log2(math.e) / math.sqrt(HDIM)
    lane_block = lax.broadcasted_iota(jnp.int32, (1, half), 1) // BLOCK
    for side in range(2):
        own = slice(side * half, (side + 1) * half)
        halo_ref = low_ref if side == 0 else high_ref
        query = q_ref[own, :]
        parts = ((halo_ref[0], halo_ref[1]), (k_ref[own, :], v_ref[own, :]))
        origin = (
            (meta[0] * blocks + (-(blocks // 2) if side == 0 else blocks)),
            meta[0] * blocks + side * (blocks // 2),
        )
        scores = []
        for (keys, _), start in zip(parts, origin):
            raw = dot(keys, query, ((1,), (1,))) * scale
            slabs = []
            for kb in range(blocks // 2):
                bias = jnp.full((1, half), EXCLUDED, F32)
                for qb in range(blocks // 2):
                    first = meta[3 + side * (blocks // 2) + qb]
                    last = meta[3 + blocks + side * (blocks // 2) + qb]
                    block = start + kb
                    inside = (block >= first) & (block < last)
                    bias = jnp.where(lane_block == qb, jnp.where(inside, 0.0, EXCLUDED), bias)
                slabs.append(raw[kb * BLOCK : (kb + 1) * BLOCK, :] + bias)
            scores.append(jnp.concatenate(slabs, axis=0))
        highest = jnp.maximum(
            jnp.max(scores[0], axis=0, keepdims=True), jnp.max(scores[1], axis=0, keepdims=True)
        )
        raised = [jnp.exp2(s - highest) for s in scores]
        total = jnp.sum(raised[0], axis=0, keepdims=True) + jnp.sum(raised[1], axis=0, keepdims=True)
        inverse = 1.0 / total
        attended = None
        for part in range(2):
            weights = (raised[part] * inverse).astype(BF16)
            prob_ref[0, side, part] = weights
            term = dot(parts[part][1], weights, ((0,), (0,)))
            attended = term if attended is None else attended + term
        attn_ref[0, :, own] = attended.astype(BF16)


def forward(meta, q, k, v, low, high, parity):
    rows, width = q.shape
    half = rows // 2
    pairs = width // HDIM // 2
    column = lambda h, m: (0, 2 * h + parity)
    halo = pl.BlockSpec((2, half, HDIM), lambda h, m: (0, 0, h))
    return pl.pallas_call(
        forward_kernel,
        grid_spec=pltpu.PrefetchScalarGridSpec(
            num_scalar_prefetch=1,
            grid=(pairs,),
            in_specs=[
                pl.BlockSpec((rows, HDIM), column),
                pl.BlockSpec((rows, HDIM), column),
                pl.BlockSpec((rows, HDIM), column),
                halo,
                halo,
            ],
            out_specs=[
                pl.BlockSpec((1, HDIM, rows), lambda h, m: (h ^ m[2], 0, 0)),
                pl.BlockSpec((1, 2, 2, half, half), lambda h, m: (h, 0, 0, 0, 0)),
            ],
        ),
        out_shape=[
            jax.ShapeDtypeStruct((pairs, HDIM, rows), BF16),
            jax.ShapeDtypeStruct((pairs, 2, 2, half, half), BF16),
        ],
        cost_estimate=pl.CostEstimate(
            flops=pairs * 8 * rows * rows * HDIM, bytes_accessed=6 << 20, transcendentals=pairs * rows * rows
        ),
        name=f"forward_{parity}",
    )(meta, q, k, v, low, high)


def weight_kernel(meta, attn_ref, dy_ref, out_ref):
    pairs, width, rows = attn_ref.shape
    columns = dy_ref.shape[1]
    product = dot(attn_ref[...].reshape(pairs * width, rows), dy_ref[...], ((1,), (0,)))
    out_ref[...] = product.astype(BF16).reshape(1, pairs, width, columns)


def weight_part(meta, attn, dy, odd, name):
    pairs, width, rows = attn.shape
    columns = dy.shape[1] // 4
    return pl.pallas_call(
        weight_kernel,
        grid_spec=pltpu.PrefetchScalarGridSpec(
            num_scalar_prefetch=1,
            grid=(2,),
            in_specs=[
                whole(attn.shape),
                pl.BlockSpec((rows, columns), lambda j, m: (0, m[1] ^ (2 * j + odd))),
            ],
            out_specs=pl.BlockSpec((1, pairs, width, columns), lambda j, m: (j, 0, 0, 0)),
        ),
        out_shape=jax.ShapeDtypeStruct((2, pairs, width, columns), BF16),
        cost_estimate=pl.CostEstimate(
            flops=4 * pairs * width * rows * columns, bytes_accessed=4 << 20, transcendentals=0
        ),
        name=name,
    )(meta, attn, dy)


def backward_kernel(aliased, meta, *refs):
    (q_ref, k_ref, v_ref, low_ref, high_ref, prob_ref, dy_ref, own_w, far_w, near_w) = refs[:10]
    refs = refs[10 + 3 * aliased :]
    dq_ref, dk_ref, dv_ref, dlow_ref, dhigh_ref, grad_scr = refs
    rows = q_ref.shape[0]
    half = rows // 2
    pairs, width, columns = own_w.shape
    head = pl.program_id(0)

    @pl.when(head == 0)
    def _():
        total = None
        for j, part in ((0, own_w[...]), (1, near_w[0]), (2, far_w[...]), (3, near_w[1])):
            place = pl.multiple_of((meta[1] ^ j) * columns, columns)
            term = dot(
                part.reshape(pairs * width, columns), dy_ref[:, pl.ds(place, columns)], ((1,), (1,))
            )
            total = term if total is None else total + term
        grad_scr[...] = total.astype(BF16).reshape(pairs, width, rows)

    relative = head ^ meta[2]
    scale = 1.0 / math.sqrt(HDIM)
    for side in range(2):
        own = slice(side * half, (side + 1) * half)
        halo_ref, dhalo_ref = (low_ref, dlow_ref) if side == 0 else (high_ref, dhigh_ref)
        query = q_ref[own, :]
        grad = grad_scr[relative, :, own]
        keys = (halo_ref[0], k_ref[own, :])
        values = (halo_ref[1], v_ref[own, :])
        probs = [prob_ref[0, side, part] for part in range(2)]
        dprobs = [dot(values[part], grad, ((1,), (0,))) for part in range(2)]
        wide = [p.astype(F32) for p in probs]
        row_term = jnp.sum(wide[0] * dprobs[0], axis=0, keepdims=True) + jnp.sum(
            wide[1] * dprobs[1], axis=0, keepdims=True
        )
        dquery = None
        for part in range(2):
            dscores = (wide[part] * ((dprobs[part] - row_term) * scale)).astype(BF16)
            term = dot(keys[part], dscores, ((0,), (0,)))
            dquery = term if dquery is None else dquery + term
            dkey = dot(dscores, query, ((1,), (0,))).astype(BF16)
            dvalue = dot(probs[part], grad, ((1,), (1,))).astype(BF16)
            if part == 0:
                dhalo_ref[0] = dkey
                dhalo_ref[1] = dvalue
            else:
                dk_ref[own, :] = dkey
                dv_ref[own, :] = dvalue
        dq_ref[own, :] = dquery.T.astype(BF16)


def backward(meta, q, k, v, low, high, prob, dy, weights, parity, previous):
    rows, width = q.shape
    half = rows // 2
    own_w, far_w, near_w = weights
    pairs, head_rows, columns = own_w.shape
    column = pl.BlockSpec((rows, HDIM), lambda h, m: (0, 2 * h + parity))
    halo = pl.BlockSpec((2, half, HDIM), lambda h, m: (0, 0, h))
    single = lambda a: pl.BlockSpec(a.shape, lambda *_: (0,) * a.ndim, pipeline_mode=pl.Buffered(1))
    aliased = previous is not None
    full = jax.ShapeDtypeStruct((rows, width), BF16)
    side = jax.ShapeDtypeStruct((2, half, width // 2), BF16)
    return pl.pallas_call(
        functools.partial(backward_kernel, aliased),
        grid_spec=pltpu.PrefetchScalarGridSpec(
            num_scalar_prefetch=1,
            grid=(pairs,),
            in_specs=[
                column,
                column,
                column,
                halo,
                halo,
                pl.BlockSpec((1, 2, 2, half, half), lambda h, m: (h, 0, 0, 0, 0)),
                single(dy),
                single(own_w),
                single(far_w),
                single(near_w),
            ]
            + [pl.BlockSpec(memory_space=pl.ANY)] * (3 * aliased),
            out_specs=[column, column, column, halo, halo],
            scratch_shapes=[pltpu.VMEM((pairs, head_rows, rows), BF16)],
        ),
        out_shape=[full, full, full, side, side],
        input_output_aliases={11: 0, 12: 1, 13: 2} if aliased else {},
        cost_estimate=pl.CostEstimate(
            flops=pairs * (16 * rows * rows * HDIM + 8 * rows * head_rows * columns),
            bytes_accessed=10 << 20,
            transcendentals=0,
        ),
        name=f"backward_{parity}",
    )(meta, q, k, v, low, high, prob, dy, own_w, far_w, near_w, *(previous or ()))


def layer_kernel(meta, attn_even, attn_odd, *refs):
    out_ref = refs[-1]
    groups = ((attn_even, refs[0:3]), (attn_odd, refs[3:6]))
    turned = []
    for attn, (own_w, far_w, near_w) in groups:
        pairs, width, rows = attn.shape
        turned.append(attn[...].reshape(pairs * width, rows).T)
    for j in range(4):
        total = None
        for lhs, (attn, (own_w, far_w, near_w)) in zip(turned, groups):
            part = (own_w[...], near_w[0], far_w[...], near_w[1])[j]
            pairs, width, columns = part.shape
            term = dot(lhs, part.reshape(pairs * width, columns), ((1,), (0,)))
            total = term if total is None else total + term
        place = pl.multiple_of((meta[1] ^ j) * columns, columns)
        out_ref[:, pl.ds(place, columns)] = total.astype(BF16)


def layer_output(meta, attn_even, attn_odd, even_w, odd_w):
    pairs, width, rows = attn_even.shape
    columns = even_w[0].shape[-1]
    half = rows // 2
    single = lambda a: pl.BlockSpec(a.shape, lambda *_: (0,) * a.ndim, pipeline_mode=pl.Buffered(1))
    attn = pl.BlockSpec((pairs, width, half), lambda t, m: (0, 0, t))
    return pl.pallas_call(
        layer_kernel,
        grid_spec=pltpu.PrefetchScalarGridSpec(
            num_scalar_prefetch=1,
            grid=(2,),
            in_specs=[attn, attn] + [single(a) for a in (*even_w, *odd_w)],
            out_specs=pl.BlockSpec((half, 4 * columns), lambda t, m: (t, 0)),
        ),
        out_shape=jax.ShapeDtypeStruct((rows, 4 * columns), BF16),
        cost_estimate=pl.CostEstimate(
            flops=16 * pairs * width * rows * columns, bytes_accessed=7 << 20, transcendentals=0
        ),
        name="layer_out",
    )(meta, attn_even, attn_odd, *even_w, *odd_w)


def merge_kernel(dk_ref, dv_ref, low_ref, high_ref, dk_out, dv_out):
    half = low_ref.shape[1]
    for index, (source, target) in enumerate(((dk_ref, dk_out), (dv_ref, dv_out))):
        for side, halo in ((0, low_ref), (1, high_ref)):
            own = slice(side * half, (side + 1) * half)
            target[own, :] = (source[own, :].astype(F32) + halo[index].astype(F32)).astype(BF16)


def merge(dk, dv, low, high, parity):
    rows, width = dk.shape
    column = pl.BlockSpec((rows, HDIM), lambda h: (0, 2 * h + parity))
    halo = pl.BlockSpec((2, rows // 2, HDIM), lambda h: (0, 0, h))
    full = jax.ShapeDtypeStruct((rows, width), BF16)
    return pl.pallas_call(
        merge_kernel,
        grid=(width // HDIM // 2,),
        in_specs=[column, column, halo, halo],
        out_specs=[column, column],
        out_shape=[full, full],
        input_output_aliases={0: 0, 1: 1},
        cost_estimate=pl.CostEstimate(flops=rows * width, bytes_accessed=3 << 20, transcendentals=0),
        name=f"merge_{parity}",
    )(dk, dv, low, high)


def pick(parity_bit, even, odd):
    return jnp.where(parity_bit == 0, even, odd)


def body(queries, memory_keys, memory_values, out_weight, grad_out, key_first, key_last):
    q, k, v, dy = queries[0], memory_keys[0], memory_values[0], grad_out[0]
    rows, width = q.shape
    half = rows // 2
    model = dy.shape[1]
    heads = width // HDIM
    pairs = heads // 2
    seq_count, dp_count = lax.axis_size("seq"), lax.axis_size("dp")
    per_head = seq_count // heads
    near, far = 1, dp_count // 2
    columns = model // dp_count
    seq = lax.axis_index("seq")
    dp = lax.axis_index("dp")
    pair = seq // (2 * per_head)
    parity = (seq // per_head) % 2
    sub = seq % per_head
    meta = jnp.concatenate(
        [jnp.stack([seq, dp, pair]).astype(jnp.int32), key_first[0], key_last[0]]
    )

    def packed(row_slice, par):
        take = lambda a: jnp.concatenate(
            [a[row_slice, (2 * h + par) * HDIM : (2 * h + par + 1) * HDIM] for h in range(pairs)], axis=1
        )
        return jnp.stack([take(k), take(v)])

    own_shard = lax.dynamic_slice_in_dim(out_weight, dp * columns, columns, 1)
    if per_head > 1:
        pieces = jnp.stack([own_shard] + [swap(own_shard, "seq", i) for i in range(1, per_head)])
        pieces = jnp.take(pieces, jnp.arange(per_head) ^ sub, axis=0)
        own_shard = pieces.reshape(HDIM, columns)
    other_shard = swap(own_shard, "seq", per_head)

    lows, highs = [], []
    for par in range(2):
        lows.append(shift(packed(slice(half, rows), par), "seq", 1))
        highs.append(shift(packed(slice(0, half), par), "seq", -1))

    weights = []
    for par in range(2):
        mine = pick(parity ^ par, own_shard, other_shard)
        gathered = jnp.stack(
            [mine] + [swap(mine, "seq", 2 * per_head * i) for i in range(1, pairs)]
        )
        across = swap(gathered, "dp", far)
        beside = swap(jnp.stack([gathered, across]), "dp", near)
        weights.append((gathered, across, beside))

    attn, prob, sums = [], [], []
    for par in range(2):
        a, p = forward(meta, q, k, v, lows[par], highs[par], par)
        attn.append(a)
        prob.append(p)
        sent = swap(weight_part(meta, a, dy, 1, f"weight_send_{par}"), "dp", near)
        kept = weight_part(meta, a, dy, 0, f"weight_keep_{par}")
        added = [(kept[i].astype(F32) + sent[i].astype(F32)) for i in range(2)]
        crossed = swap(added[1].astype(BF16), "dp", far)
        total = added[0] + crossed.astype(F32)
        result = total[0]
        for i in range(1, pairs):
            result = result + swap(total[i].astype(BF16), "seq", 2 * per_head * i).astype(F32)
        sums.append(result)

    previous = None
    from_low, from_high = [], []
    for par in range(2):
        dq, dk, dv, dlow, dhigh = backward(
            meta, q, k, v, lows[par], highs[par], prob[par], dy, weights[par], par, previous
        )
        previous = (dq, dk, dv)
        from_high.append(shift(dlow, "seq", -1))
        from_low.append(shift(dhigh, "seq", 1))

    layer_out = layer_output(meta, attn[0], attn[1], weights[0], weights[1])

    theirs = pick(parity, sums[1], sums[0]).astype(BF16)
    total = pick(parity, sums[0], sums[1]) + swap(theirs, "seq", per_head).astype(F32)
    if per_head > 1:
        split = total.reshape(per_head, HDIM // per_head, columns)
        split = jnp.take(split, jnp.arange(per_head) ^ sub, axis=0)
        total = split[0]
        for i in range(1, per_head):
            total = total + swap(split[i].astype(BF16), "seq", i).astype(F32)
    mine = total.astype(BF16)
    across = swap(mine, "dp", far)
    both = jnp.stack([mine, across])
    beside = swap(both, "dp", near)
    relative = [mine, beside[0], across, beside[1]]
    straight = [pick(dp & near, relative[i], relative[i ^ near]) for i in range(4)]
    placed = [pick(dp & far, straight[i], straight[i ^ far]) for i in range(4)]
    normalizer = math.sqrt(seq_count * rows)
    weight_grad = jnp.concatenate(placed, axis=1).astype(F32) / normalizer

    for par in range(2):
        dk, dv = merge(dk, dv, from_low[par], from_high[par], par)

    return (layer_out[None], dq[None], dk[None], dv[None], weight_grad)


def solution(mesh):
    rows = P("dp", "seq", None)
    return jax.shard_map(
        body,
        mesh=mesh,
        in_specs=(rows, rows, rows, P("seq", None), rows, P("dp", "seq"), P("dp", "seq")),
        out_specs=(rows, rows, rows, rows, P("seq", None)),
        check_vma=False,
    )
```

```python
import functools
import math

import jax
import jax.numpy as jnp
from jax import lax
from jax.experimental import pallas as pl
from jax.experimental.pallas import tpu as pltpu
from jax.sharding import PartitionSpec as P


HDIM = 128
BLOCK = 128
BF16 = jnp.bfloat16
F32 = jnp.float32
EXCLUDED = -1e30
VMEM_LIMIT = 20 << 20


def dot(a, b, contract):
    return lax.dot_general(a, b, ((contract[0], contract[1]), ((), ())), preferred_element_type=F32)


def swap(block, axis, mask):
    pairs = [(i, i ^ mask) for i in range(lax.axis_size(axis))]
    return lax.ppermute(block, axis, pairs)


def exchange(block, axis, near):
    count = lax.axis_size(axis)
    lower = range(0 if near else 1, count - 1, 2)
    return lax.ppermute(block, axis, [p for i in lower for p in ((i, i + 1), (i + 1, i))])


def whole(shape):
    return pl.BlockSpec(shape, lambda *_: (0,) * len(shape))


def side_of(meta, relative, half):
    side = meta[3] ^ 1 ^ relative
    return side, pl.ds(pl.multiple_of(side * half, half), half)


def pack_kernel(meta, k_ref, v_ref, *outs):
    half = k_ref.shape[0] // 2
    for part in range(2):
        lanes = pl.ds(pl.multiple_of((meta[3] ^ part) * HDIM, HDIM), HDIM)
        for index, ref in enumerate((k_ref, v_ref)):
            for side in range(2):
                outs[2 * part + side][index] = ref[side_of(meta, side, half)[1], lanes]


def pack(meta, k, v):
    rows, width = k.shape
    block = pl.BlockSpec((rows, 2 * HDIM), lambda h, m: (0, h))
    out = pl.BlockSpec((2, rows // 2, HDIM), lambda h, m: (0, 0, h))
    return pl.pallas_call(
        pack_kernel,
        grid_spec=pltpu.PrefetchScalarGridSpec(
            num_scalar_prefetch=1,
            grid=(width // HDIM // 2,),
            in_specs=[block, block],
            out_specs=[out] * 4,
        ),
        out_shape=[jax.ShapeDtypeStruct((2, rows // 2, width // 2), BF16)] * 4,
        compiler_params=pltpu.CompilerParams(vmem_limit_bytes=VMEM_LIMIT),
        cost_estimate=pl.CostEstimate(flops=0, bytes_accessed=4 << 20, transcendentals=0),
        name="kp",
    )(meta, k, v)


def forward_kernel(
    meta, q_ref, k_ref, v_ref, knear_ref, vnear_ref, kfar_ref, vfar_ref, attn_ref, prob_ref
):
    rows = q_ref.shape[0]
    half = rows // 2
    blocks = rows // BLOCK
    scale = math.log2(math.e) / math.sqrt(HDIM)
    lane_block = lax.broadcasted_iota(jnp.int32, (1, half), 1) // BLOCK
    sides = []
    for side in range(2):
        own = side_of(meta, side, half)[1]
        khalo_ref, vhalo_ref = ((knear_ref, vnear_ref), (kfar_ref, vfar_ref))[side]
        query = q_ref[own, :]
        raw = [dot(keys, query, ((1,), (1,))) for keys in (khalo_ref[...], k_ref[own, :])]
        sides.append((own, (vhalo_ref[...], v_ref[own, :]), raw))
    scored = []
    for side, (_, _, raw) in enumerate(sides):
        place = side_of(meta, side, half)[0]
        reach = blocks // 2
        origin = (
            meta[0] * blocks - reach + place * (blocks + reach),
            meta[0] * blocks + place * reach,
        )
        scores = []
        for part, start in zip(raw, origin):
            slabs = []
            for kb in range(blocks // 2):
                bias = jnp.full((1, half), EXCLUDED, F32)
                for qb in range(blocks // 2):
                    first = meta[4 + place * reach + qb]
                    last = meta[4 + blocks + place * reach + qb]
                    block = start + kb
                    inside = (block >= first) & (block < last)
                    bias = jnp.where(lane_block == qb, jnp.where(inside, 0.0, EXCLUDED), bias)
                slabs.append(part[kb * BLOCK : (kb + 1) * BLOCK, :] * scale + bias)
            scores.append(jnp.concatenate(slabs, axis=0))
        highest = jnp.maximum(
            jnp.max(scores[0], axis=0, keepdims=True), jnp.max(scores[1], axis=0, keepdims=True)
        )
        scored.append((scores, highest))
    for side, ((own, values, _), (scores, highest)) in enumerate(zip(sides, scored)):
        raised = [jnp.exp2(s - highest) for s in scores]
        total = jnp.sum(raised[0], axis=0, keepdims=True) + jnp.sum(raised[1], axis=0, keepdims=True)
        inverse = 1.0 / total
        attended = None
        for part in range(2):
            weights = (raised[part] * inverse).astype(BF16)
            prob_ref[0, side, part] = weights
            term = dot(values[part], weights, ((0,), (0,)))
            attended = term if attended is None else attended + term
        attn_ref[0, :, own] = attended.astype(BF16)


def forward(meta, q, k, v, near, far, part):
    rows, width = q.shape
    half = rows // 2
    pairs = width // HDIM // 2
    column = lambda h, m: (0, 2 * h + (m[3] ^ 1 ^ part))
    halo_key = pl.BlockSpec((None, half, HDIM), lambda h, m: (0, 0, h))
    halo_value = pl.BlockSpec((None, half, HDIM), lambda h, m: (1, 0, h))
    return pl.pallas_call(
        forward_kernel,
        grid_spec=pltpu.PrefetchScalarGridSpec(
            num_scalar_prefetch=1,
            grid=(pairs,),
            in_specs=[
                pl.BlockSpec((rows, HDIM), column),
                pl.BlockSpec((rows, HDIM), column),
                pl.BlockSpec((rows, HDIM), column),
                halo_key,
                halo_value,
                halo_key,
                halo_value,
            ],
            out_specs=[
                pl.BlockSpec((1, HDIM, rows), lambda h, m: (h ^ m[2], 0, 0)),
                pl.BlockSpec((1, 2, 2, half, half), lambda h, m: (h, 0, 0, 0, 0)),
            ],
        ),
        out_shape=[
            jax.ShapeDtypeStruct((pairs, HDIM, rows), BF16),
            jax.ShapeDtypeStruct((pairs, 2, 2, half, half), BF16),
        ],
        compiler_params=pltpu.CompilerParams(vmem_limit_bytes=VMEM_LIMIT),
        cost_estimate=pl.CostEstimate(
            flops=pairs * 8 * rows * rows * HDIM, bytes_accessed=6 << 20, transcendentals=pairs * rows * rows
        ),
    )(meta, q, k, v, near, near, far, far)


def weight_kernel(meta, attn_ref, dy_ref, out_ref):
    pairs, width, rows = attn_ref.shape
    columns = dy_ref.shape[1]
    product = dot(attn_ref[...].reshape(pairs * width, rows), dy_ref[...], ((1,), (0,)))
    out_ref[...] = product.astype(BF16).reshape(1, pairs, width, columns)


def weight_part(meta, attn, dy, odd):
    pairs, width, rows = attn.shape
    columns = dy.shape[1] // 4
    return pl.pallas_call(
        weight_kernel,
        grid_spec=pltpu.PrefetchScalarGridSpec(
            num_scalar_prefetch=1,
            grid=(2,),
            in_specs=[
                whole(attn.shape),
                pl.BlockSpec((rows, columns), lambda j, m: (0, m[1] ^ (2 * j + odd))),
            ],
            out_specs=pl.BlockSpec((1, pairs, width, columns), lambda j, m: (j, 0, 0, 0)),
        ),
        out_shape=jax.ShapeDtypeStruct((2, pairs, width, columns), BF16),
        compiler_params=pltpu.CompilerParams(vmem_limit_bytes=VMEM_LIMIT),
        cost_estimate=pl.CostEstimate(
            flops=4 * pairs * width * rows * columns, bytes_accessed=4 << 20, transcendentals=0
        ),
    )(meta, attn, dy)


def grad_kernel(meta, dy_ref, own_w, far_w, near_w, out_ref):
    pairs, width, columns = own_w.shape
    total = None
    for j, part in ((0, own_w[...]), (1, near_w[0]), (2, far_w[...]), (3, near_w[1])):
        place = pl.multiple_of((meta[1] ^ j) * columns, columns)
        term = dot(part.reshape(pairs * width, columns), dy_ref[:, pl.ds(place, columns)], ((1,), (1,)))
        total = term if total is None else total + term
    out_ref[...] = total.astype(BF16).reshape(out_ref.shape)


def grad_attention(meta, dy, weights):
    pairs, width, columns = weights[0].shape
    rows = dy.shape[0]
    single = lambda a: pl.BlockSpec(a.shape, lambda *_: (0,) * a.ndim)
    return pl.pallas_call(
        grad_kernel,
        grid_spec=pltpu.PrefetchScalarGridSpec(
            num_scalar_prefetch=1,
            grid=(1,),
            in_specs=[single(dy)] + [single(a) for a in weights],
            out_specs=pl.BlockSpec((pairs, width, rows), lambda *_: (0, 0, 0)),
        ),
        out_shape=jax.ShapeDtypeStruct((pairs, width, rows), BF16),
        compiler_params=pltpu.CompilerParams(vmem_limit_bytes=VMEM_LIMIT),
        cost_estimate=pl.CostEstimate(
            flops=8 * pairs * width * rows * columns, bytes_accessed=4 << 20, transcendentals=0
        ),
    )(meta, dy, *weights)


def backward_kernel(aliased, meta, *refs):
    q_ref, k_ref, v_ref, knear_ref, vnear_ref, kfar_ref, vfar_ref, prob_ref, grad_ref = refs[:9]
    dq_ref, dk_ref, dv_ref, dnear_ref, dfar_ref = refs[9 + aliased :]
    half = q_ref.shape[0] // 2
    scale = 1.0 / math.sqrt(HDIM)
    sides = []
    for side in range(2):
        own = side_of(meta, side, half)[1]
        vhalo_ref = (vnear_ref, vfar_ref)[side]
        grad = grad_ref[0, :, own]
        dprobs = [dot(value, grad, ((1,), (0,))) for value in (vhalo_ref[...], v_ref[own, :])]
        sides.append((own, grad, dprobs))
    for side, (own, grad, _) in enumerate(sides):
        for part, (ref, place) in enumerate((((dnear_ref, dfar_ref)[side], None), (dv_ref, own))):
            dvalue = dot(prob_ref[0, side, part], grad, ((1,), (1,))).astype(BF16)
            if place is None:
                ref[1] = dvalue
            else:
                ref[place, :] = dvalue
    scored = []
    for side, (_, _, dprobs) in enumerate(sides):
        wide = [prob_ref[0, side, part].astype(F32) for part in range(2)]
        row_term = jnp.sum(wide[0] * dprobs[0], axis=0, keepdims=True) + jnp.sum(
            wide[1] * dprobs[1], axis=0, keepdims=True
        )
        scored.append(
            [(wide[part] * ((dprobs[part] - row_term) * scale)).astype(BF16) for part in range(2)]
        )
    for side, ((own, _, _), dscores) in enumerate(zip(sides, scored)):
        khalo_ref = (knear_ref, kfar_ref)[side]
        query = q_ref[own, :]
        (dnear_ref, dfar_ref)[side][0] = dot(dscores[0], query, ((1,), (0,))).astype(BF16)
        dk_ref[own, :] = dot(dscores[1], query, ((1,), (0,))).astype(BF16)
        dquery = dot(khalo_ref[...], dscores[0], ((0,), (0,))) + dot(
            k_ref[own, :], dscores[1], ((0,), (0,))
        )
        dq_ref[own, :] = dquery.astype(BF16).T


def backward(meta, q, k, v, near, far, prob, grad, part, previous):
    rows, width = q.shape
    half = rows // 2
    pairs = grad.shape[0]
    column = pl.BlockSpec((rows, HDIM), lambda h, m: (0, 2 * h + (m[3] ^ 1 ^ part)))
    chunk = pl.BlockSpec((rows, HDIM), lambda h, m: (0, h))
    halo = pl.BlockSpec((2, half, HDIM), lambda h, m: (0, 0, h))
    halo_key = pl.BlockSpec((None, half, HDIM), lambda h, m: (0, 0, h))
    halo_value = pl.BlockSpec((None, half, HDIM), lambda h, m: (1, 0, h))
    aliased = previous is not None
    full = jax.ShapeDtypeStruct((rows, width), BF16)
    own = jax.ShapeDtypeStruct((rows, width // 2), BF16)
    side = jax.ShapeDtypeStruct((2, half, width // 2), BF16)
    return pl.pallas_call(
        functools.partial(backward_kernel, aliased),
        grid_spec=pltpu.PrefetchScalarGridSpec(
            num_scalar_prefetch=1,
            grid=(pairs,),
            in_specs=[
                column,
                column,
                column,
                halo_key,
                halo_value,
                halo_key,
                halo_value,
                pl.BlockSpec((1, 2, 2, half, half), lambda h, m: (h, 0, 0, 0, 0)),
                pl.BlockSpec((1, HDIM, rows), lambda h, m: (h ^ m[2], 0, 0)),
            ]
            + [pl.BlockSpec(memory_space=pl.ANY)] * aliased,
            out_specs=[column, chunk, chunk, halo, halo],
        ),
        out_shape=[full, own, own, side, side],
        input_output_aliases={10: 0} if aliased else {},
        compiler_params=pltpu.CompilerParams(vmem_limit_bytes=VMEM_LIMIT),
        cost_estimate=pl.CostEstimate(
            flops=16 * pairs * rows * rows * HDIM, bytes_accessed=10 << 20, transcendentals=0
        ),
    )(meta, q, k, v, near, near, far, far, prob, grad, *((previous,) if aliased else ()))


def layer_kernel(meta, attn_0, attn_1, *refs):
    out_ref = refs[-1]
    groups = ((attn_0, refs[0:3]), (attn_1, refs[3:6]))
    turned = []
    for attn, (own_w, far_w, near_w) in groups:
        pairs, width, rows = attn.shape
        turned.append(attn[...].reshape(pairs * width, rows).T)
    for j in range(4):
        total = None
        for lhs, (attn, (own_w, far_w, near_w)) in zip(turned, groups):
            part = (own_w[...], near_w[0], far_w[...], near_w[1])[j]
            pairs, width, columns = part.shape
            term = dot(lhs, part.reshape(pairs * width, columns), ((1,), (0,)))
            total = term if total is None else total + term
        place = pl.multiple_of((meta[1] ^ j) * columns, columns)
        out_ref[:, pl.ds(place, columns)] = total.astype(BF16)


def layer_output(meta, attn_0, attn_1, weights_0, weights_1):
    pairs, width, rows = attn_0.shape
    columns = weights_0[0].shape[-1]
    half = rows // 2
    single = lambda a: pl.BlockSpec(a.shape, lambda *_: (0,) * a.ndim, pipeline_mode=pl.Buffered(1))
    attn = pl.BlockSpec((pairs, width, half), lambda t, m: (0, 0, t))
    return pl.pallas_call(
        layer_kernel,
        grid_spec=pltpu.PrefetchScalarGridSpec(
            num_scalar_prefetch=1,
            grid=(2,),
            in_specs=[attn, attn] + [single(a) for a in (*weights_0, *weights_1)],
            out_specs=pl.BlockSpec((half, 4 * columns), lambda t, m: (t, 0)),
        ),
        out_shape=jax.ShapeDtypeStruct((rows, 4 * columns), BF16),
        compiler_params=pltpu.CompilerParams(vmem_limit_bytes=VMEM_LIMIT),
        cost_estimate=pl.CostEstimate(
            flops=16 * pairs * width * rows * columns, bytes_accessed=7 << 20, transcendentals=0
        ),
        name="kl",
    )(meta, attn_0, attn_1, *weights_0, *weights_1)


def merge_kernel(meta, dk_ref, dv_ref, near_ref, far_ref, *refs):
    half = near_ref.shape[1]
    for index, (source, target) in enumerate(zip((dk_ref, dv_ref), refs[-2:])):
        for side, halo in ((0, near_ref), (1, far_ref)):
            own = side_of(meta, side, half)[1]
            target[own, :] = (source[own, :].astype(F32) + halo[index].astype(F32)).astype(BF16)


def merge(meta, dk, dv, near, far, part, previous):
    rows, width = dk.shape
    aliased = previous is not None
    chunk = pl.BlockSpec((rows, HDIM), lambda h, m: (0, h))
    column = pl.BlockSpec((rows, HDIM), lambda h, m: (0, 2 * h + (m[3] ^ 1 ^ part)))
    halo = pl.BlockSpec((2, rows // 2, HDIM), lambda h, m: (0, 0, h))
    full = jax.ShapeDtypeStruct((rows, 2 * width), BF16)
    return pl.pallas_call(
        merge_kernel,
        grid_spec=pltpu.PrefetchScalarGridSpec(
            num_scalar_prefetch=1,
            grid=(width // HDIM,),
            in_specs=[chunk, chunk, halo, halo] + [pl.BlockSpec(memory_space=pl.ANY)] * (2 * aliased),
            out_specs=[column, column],
        ),
        out_shape=[full, full],
        input_output_aliases={5: 0, 6: 1} if aliased else {},
        compiler_params=pltpu.CompilerParams(vmem_limit_bytes=VMEM_LIMIT),
        cost_estimate=pl.CostEstimate(
            flops=2 * rows * width, bytes_accessed=3 << 20, transcendentals=0
        ),
    )(meta, dk, dv, near, far, *(previous or ()))


def place_kernel(factor, meta, own_ref, far_ref, near_ref, out_ref):
    columns = own_ref.shape[1]
    for j, part in ((0, own_ref[...]), (1, near_ref[0]), (2, far_ref[...]), (3, near_ref[1])):
        start = pl.multiple_of((meta[1] ^ j) * columns, columns)
        out_ref[:, pl.ds(start, columns)] = part.astype(F32) * factor


def place(meta, own, far, near, factor):
    rows, columns = own.shape
    single = lambda a: pl.BlockSpec(a.shape, lambda *_: (0,) * a.ndim)
    return pl.pallas_call(
        functools.partial(place_kernel, factor),
        grid_spec=pltpu.PrefetchScalarGridSpec(
            num_scalar_prefetch=1,
            grid=(1,),
            in_specs=[single(own), single(far), single(near)],
            out_specs=pl.BlockSpec((rows, 4 * columns), lambda *_: (0, 0)),
        ),
        out_shape=jax.ShapeDtypeStruct((rows, 4 * columns), F32),
        compiler_params=pltpu.CompilerParams(vmem_limit_bytes=VMEM_LIMIT),
        cost_estimate=pl.CostEstimate(flops=4 * rows * columns, bytes_accessed=2 << 20, transcendentals=0),
        name="ke",
    )(meta, own, far, near)


def pick(parity_bit, even, odd):
    return jnp.where(parity_bit == 0, even, odd)


def body(queries, memory_keys, memory_values, out_weight, grad_out, key_first, key_last):
    q, k, v, dy = queries[0], memory_keys[0], memory_values[0], grad_out[0]
    rows, width = q.shape
    model = dy.shape[1]
    heads = width // HDIM
    pairs = heads // 2
    seq_count, dp_count = lax.axis_size("seq"), lax.axis_size("dp")
    per_head = seq_count // heads
    near, far = 1, dp_count // 2
    columns = model // dp_count
    seq = lax.axis_index("seq")
    dp = lax.axis_index("dp")
    pair = seq // (2 * per_head)
    odd = seq % 2
    turned = ((seq // per_head) ^ seq) & 1
    sub = seq % per_head
    meta = jnp.concatenate(
        [jnp.stack([seq, dp, pair, odd]).astype(jnp.int32), key_first[0], key_last[0]]
    )

    own_shard = lax.dynamic_slice_in_dim(out_weight, dp * columns, columns, 1)
    if per_head > 1:
        pieces = jnp.stack([own_shard] + [swap(own_shard, "seq", i) for i in range(1, per_head)])
        pieces = jnp.take(pieces, jnp.arange(per_head) ^ sub, axis=0)
        own_shard = pieces.reshape(HDIM, columns)
    other_shard = swap(own_shard, "seq", per_head)

    packed = pack(meta, k, v)
    nears = [exchange(packed[2 * part], "seq", True) for part in range(2)]
    fars = [exchange(packed[2 * part + 1], "seq", False) for part in range(2)]

    def ordered(other, own):
        if per_head == 1:
            return other, own
        return pick(turned, other, own), pick(turned, own, other)

    weights = []
    for shard in ordered(other_shard, own_shard):
        gathered = jnp.stack(
            [shard]
            + [swap(shard, "seq", 2 * per_head * i) for i in range(1, pairs)]
        )
        across = swap(gathered, "dp", far)
        beside = swap(jnp.stack([gathered, across]), "dp", near)
        weights.append((gathered, across, beside))

    attn, prob, sums = [], [], []
    for part in range(2):
        a, p = forward(meta, q, k, v, nears[part], fars[part], part)
        attn.append(a)
        prob.append(p)
        sent = swap(weight_part(meta, a, dy, 1), "dp", near)
        kept = weight_part(meta, a, dy, 0)
        added = [(kept[i].astype(F32) + sent[i].astype(F32)) for i in range(2)]
        crossed = swap(added[1].astype(BF16), "dp", far)
        total = added[0] + crossed.astype(F32)
        result = total[0]
        for i in range(1, pairs):
            result = result + swap(total[i].astype(BF16), "seq", 2 * per_head * i).astype(F32)
        sums.append(result)

    grads = [grad_attention(meta, dy, weights[part]) for part in range(2)]
    dq = None
    own, from_near, from_far = [], [], []
    for part in range(2):
        dq, dk, dv, dnear, dfar = backward(
            meta, q, k, v, nears[part], fars[part], prob[part], grads[part], part, dq
        )
        own.append((dk, dv))
        from_near.append(exchange(dnear, "seq", True))
        from_far.append(exchange(dfar, "seq", False))

    layer_out = layer_output(meta, attn[0], attn[1], weights[0], weights[1])

    other_sum, own_sum = ordered(*sums)
    total = own_sum + swap(other_sum.astype(BF16), "seq", per_head).astype(F32)
    if per_head > 1:
        split = total.reshape(per_head, HDIM // per_head, columns)
        split = jnp.take(split, jnp.arange(per_head) ^ sub, axis=0)
        total = split[0]
        for i in range(1, per_head):
            total = total + swap(split[i].astype(BF16), "seq", i).astype(F32)
    mine = total.astype(BF16)
    across = swap(mine, "dp", far)
    both = jnp.stack([mine, across])
    beside = swap(both, "dp", near)
    weight_grad = place(meta, mine, across, beside, 1.0 / math.sqrt(seq_count * rows))

    merged = None
    for part in (1, 0):
        merged = merge(meta, *own[part], from_near[1 - part], from_far[1 - part], part, merged)
    dk, dv = merged

    return (layer_out[None], dq[None], dk[None], dv[None], weight_grad)


def solution(mesh):
    rows = P("dp", "seq", None)


    return jax.shard_map(
        body,
        mesh=mesh,
        in_specs=(rows, rows, rows, P("seq", None), rows, P("dp", "seq"), P("dp", "seq")),
        out_specs=(rows, rows, rows, rows, P("seq", None)),
        check_vma=False,
    )
```
